32 devices in a mesh: depth: 8 (over z, y), lat: 4 (over x, core).
Axes of the slice: x: 2, y: 2, z: 4, core: 2. Of those that a mesh axis runs over, the one named last changes fastest.
Arguments:
- incident: float32 [8, 2, 2, 128, 128], P('depth', None, None, 'lat'), may hold values from -6 to 6
- contrast: float32 [8, 128, 128], P('depth', 'lat'), may hold values from -0.8 to 0.8
- kernel: bfloat16 [8, 8, 2, 256, 256], P('depth', None, None, 'lat'), may hold values from -6 to 6
Outputs:
- total_field: float32 [8, 2, 2, 128, 128], P('depth', None, None, 'lat')
The draws below stay inside these ranges and needn't reach their ends.
All inputs are finite; a program needn't handle non-finite values.
Results may differ from the reference program's by a relative error of at most 0.017.
Values may be sent and summed in bfloat16 or wider, within the bound.
A program may use at most 64 MiB of HBM per device.

```python
import math
import jax
import jax.numpy as jnp
from jax import lax

L = 128
SRC = 2
ITERS = 3
NZ = 8
P_SIZE = 256


def shard_levels(own_key, shape, pieces, least, top_value):
    def one(position, blocks):
        steps = jax.random.uniform(jax.random.fold_in(jax.random.fold_in(own_key, 6), position), (blocks,), jnp.float32, least / len(pieces), top_value / len(pieces))
        return jnp.repeat(jnp.exp(steps), shape[position] // blocks).reshape((-1,) + (1,) * (len(shape) - position - 1))

    factor_of = one(*pieces[0])
    for cut in pieces[1:]:
        factor_of = factor_of * one(*cut)
    return factor_of


def noise(own_key, dims, width, reach, pieces=(), held_as=jnp.bfloat16):
    array = width * jax.random.normal(own_key, dims, jnp.float32)
    if pieces:
        array = array * shard_levels(own_key, dims, pieces, -0.22, 0.18)
    return jnp.clip(array, -reach, reach).astype(held_as)


def setup_inputs(seed: int = 0) -> dict:
    streams_of = jax.random.split(jax.random.key(seed), 4)
    return {
        "incident": noise(streams_of[0], (NZ, SRC, 2, L, L), 1.0, 6.0, ((0, 8), (3, 4)), jnp.float32),
        "contrast": jnp.clip(jax.random.uniform(streams_of[1], (NZ, L, L), jnp.float32, -0.8, 0.8) * shard_levels(streams_of[1], (NZ, L, L), ((0, 8), (1, 4)), -0.4, 0.0), -0.8, 0.8),
        "kernel": noise(streams_of[2], (NZ, NZ, 2, P_SIZE, P_SIZE), (3.0 / NZ ** 0.5), 6.0, ((0, 8), (3, 4))),
    }


def wave_tables(count_in, count_out, period):
    indices = (jnp.arange(count_in, dtype=jnp.int32)[:, None] * jnp.arange(count_out, dtype=jnp.int32)[None, :]) % period
    angles = indices.astype(jnp.float32) * (2.0 * math.pi / period)
    return jnp.cos(angles).astype(jnp.bfloat16), jnp.sin(angles).astype(jnp.bfloat16)


def as_float(values):
    return values.astype(jnp.float32)


def last_dot(left, right):
    return jnp.einsum("...a,ab->...b", as_float(left), as_float(right), precision=lax.Precision.HIGHEST)


def middle_dot(left, right):
    return jnp.einsum("...ak,ab->...kb", as_float(left), as_float(right), precision=lax.Precision.HIGHEST)


def forward_pass(values, cosine, sine_table, product):
    real_part = values[..., 0, :, :]
    imag_part = values[..., 1, :, :]
    out_real = product(real_part, cosine) + product(imag_part, sine_table)
    out_imag = product(imag_part, cosine) - product(real_part, sine_table)
    return jnp.stack([out_real, out_imag], axis=-3)


def inverse_pass(values, cosine, sine_table, product):
    real_part = values[..., 0, :, :]
    imag_part = values[..., 1, :, :]
    out_real = product(real_part, cosine) - product(imag_part, sine_table)
    out_imag = product(real_part, sine_table) + product(imag_part, cosine)
    return jnp.stack([out_real, out_imag], axis=-3)


def couple(kern_rows, spectra):
    kern_real = kern_rows[:, :, 0]
    kern_imag = kern_rows[:, :, 1]
    spec_real = spectra[:, :, 0]
    spec_imag = spectra[:, :, 1]
    form = "lwkm,wskm->lskm"
    high = lax.Precision.HIGHEST
    out_real = jnp.einsum(form, kern_real, spec_real, precision=high) - jnp.einsum(form, kern_imag, spec_imag, precision=high)
    out_imag = jnp.einsum(form, kern_real, spec_imag, precision=high) + jnp.einsum(form, kern_imag, spec_real, precision=high)
    return jnp.stack([out_real, out_imag], axis=2)


def reference(incident, contrast, kernel):
    period = 2 * L
    forward_cos, forward_sin = wave_tables(L, period, period)
    inverse_cos, inverse_sin = wave_tables(period, L, period)
    fields = incident
    for iteration in range(ITERS):
        sources = (contrast[:, None, None] * fields).astype(jnp.bfloat16)
        along_y = forward_pass(sources, forward_cos, forward_sin, last_dot).astype(jnp.bfloat16)
        spectra = as_float(forward_pass(along_y, forward_cos, forward_sin, middle_dot).astype(jnp.bfloat16))

        def one_row(kern_row):
            return couple(as_float(kern_row)[None], spectra)[0]

        scattered = lax.map(one_row, kernel).astype(jnp.bfloat16)
        along_x = inverse_pass(scattered, inverse_cos, inverse_sin, last_dot).astype(jnp.bfloat16)
        fields = incident + inverse_pass(along_x, inverse_cos, inverse_sin, middle_dot) / float(period * period)
    return fields
```

```python
import functools
import math

import jax
import jax.numpy as jnp
import numpy as np
from jax import lax
from jax.experimental import pallas as pl
from jax.experimental.pallas import tpu as pltpu
from jax.sharding import PartitionSpec as P

L = 128
ITERS = 3
MESH = pl.DeviceIdType.MESH


def wave_tables(count_in, count_out, period):
    indices = (
        jnp.arange(count_in, dtype=jnp.int32)[:, None]
        * jnp.arange(count_out, dtype=jnp.int32)[None, :]
        % period
    )
    angles = indices.astype(jnp.float32) * (2.0 * math.pi / period)
    return (jnp.cos(angles).astype(jnp.bfloat16), jnp.sin(angles).astype(jnp.bfloat16))


def last_dot(left, right):
    return jnp.einsum("...a,ab->...b", left, right, preferred_element_type=jnp.float32)


def middle_dot(left, right):
    return jnp.einsum("...ak,ab->...kb", left, right, preferred_element_type=jnp.float32)


def forward_pass(values, cosine, sine_table, product):
    real_part = values[..., 0, :, :]
    imag_part = values[..., 1, :, :]
    out_real = product(real_part, cosine) + product(imag_part, sine_table)
    out_imag = product(imag_part, cosine) - product(real_part, sine_table)
    return jnp.stack([out_real, out_imag], axis=-3)


def inverse_pass(values, cosine, sine_table, product):
    real_part = values[..., 0, :, :]
    imag_part = values[..., 1, :, :]
    out_real = product(real_part, cosine) - product(imag_part, sine_table)
    out_imag = product(real_part, sine_table) + product(imag_part, cosine)
    return jnp.stack([out_real, out_imag], axis=-3)


def couple_grid(kern_rows, spectra):
    form = "lwkm,wskm->lskm"
    kern_real = kern_rows[:, :, 0]
    kern_imag = kern_rows[:, :, 1]
    spec_real = spectra[:, :, 0]
    spec_imag = spectra[:, :, 1]
    out_real = jnp.einsum(
        form, kern_real, spec_real, preferred_element_type=jnp.float32
    ) - jnp.einsum(form, kern_imag, spec_imag, preferred_element_type=jnp.float32)
    out_imag = jnp.einsum(
        form, kern_real, spec_imag, preferred_element_type=jnp.float32
    ) + jnp.einsum(form, kern_imag, spec_real, preferred_element_type=jnp.float32)
    return jnp.stack([out_real, out_imag], axis=2)


def local(incident, contrast, kernel):
    period = 2 * L
    forward_cos, forward_sin = wave_tables(L, period, period)
    inverse_cos, inverse_sin = wave_tables(period, L, period)
    fields = incident
    for iteration in range(ITERS):
        sources = (contrast[:, None, None] * fields).astype(jnp.bfloat16)
        along_y = forward_pass(sources, forward_cos, forward_sin, last_dot).astype(jnp.bfloat16)
        spectra = forward_pass(
            lax.all_to_all(along_y, "lat", split_axis=4, concat_axis=3, tiled=True),
            forward_cos,
            forward_sin,
            middle_dot,
        ).astype(jnp.bfloat16)
        summed = couple_grid(kernel, lax.all_gather(spectra, "depth", axis=0, tiled=True))
        scattered = summed.astype(jnp.bfloat16)
        along_x = inverse_pass(scattered, inverse_cos, inverse_sin, last_dot).astype(jnp.bfloat16)
        returned = inverse_pass(
            lax.all_to_all(along_x, "lat", split_axis=4, concat_axis=3, tiled=True),
            inverse_cos,
            inverse_sin,
            middle_dot,
        )
        fields = incident + returned / float(period * period)
    return fields


def dft(rows, columns, period):
    angles = (np.outer(np.arange(rows), np.arange(columns)) % period) * (2.0 * math.pi / period)
    return np.cos(angles), np.sin(angles)


def tables(length, lats):
    period = 2 * length
    part = length // lats
    cos_f, sin_f = dft(length, period, period)
    cos_i, sin_i = dft(period, length, period)
    forward_y = np.concatenate([cos_f.T, sin_f.T], axis=1)
    inverse_y = np.concatenate([cos_i, sin_i], axis=1)
    real_rows = np.concatenate([cos_f, -sin_f], axis=1).reshape(lats, part, 2 * period)
    imag_rows = np.concatenate([sin_f, cos_f], axis=1).reshape(lats, part, 2 * period)
    forward_x = np.stack([real_rows, imag_rows], axis=1).reshape(2 * length, 2 * period)
    to_real = np.concatenate([cos_i, -sin_i], axis=0).reshape(2 * period, lats, part)
    to_imag = np.concatenate([sin_i, cos_i], axis=0).reshape(2 * period, lats, part)
    inverse_x = np.stack([to_real, to_imag], axis=2).reshape(2 * period, 2 * length)
    return tuple(jnp.asarray(t, jnp.bfloat16) for t in (forward_y, forward_x, inverse_x, inverse_y))


def born_kernel(
    depths, lats,
    incident, contrast, green, forward_y, forward_x, inverse_x, inverse_y, out,
    slabs, out_a, in_a, out_b, in_b, spectra, scattered,
    slab_send, slab_recv, send_a, recv_a, send_b, recv_b,
):
    depth = lax.axis_index("depth")
    lat = lax.axis_index("lat")
    devices = depths * lats
    me = depth * lats + lat
    rows = out_a.shape[1]
    sources_count, _, part, length = incident.shape[1:]
    lanes = 2 * part
    period = inverse_y.shape[0]

    def peer(k):
        number = lax.rem(me + k, devices)
        return number // lats, lax.rem(number, lats)

    barrier = pltpu.get_barrier_semaphore()

    def greet(k, carry):
        pl.semaphore_signal(barrier, inc=1, device_id=peer(k), device_id_type=MESH)
        return carry

    lax.fori_loop(1, devices, greet, 0)

    own = pltpu.make_async_copy(
        green.at[0, :, :, pl.ds(pl.multiple_of(depth * rows, rows), rows)],
        slabs.at[depth],
        slab_recv.at[depth],
    )
    own.start()

    def halves(field):
        return field.reshape(sources_count, 2, part, length)

    def spread_along_y(field):
        driven = contrast[0][None, None] * halves(field)
        turned = jnp.concatenate([driven[:, 1:2], -driven[:, 0:1]], axis=1)
        flat = (sources_count * 2 * part, length)
        both = jnp.concatenate([driven.reshape(flat), turned.reshape(flat)], axis=1).astype(jnp.bfloat16)
        along_y = lax.dot_general(
            forward_y[...], both, (((1,), (1,)), ((), ())), preferred_element_type=jnp.float32
        )
        out_a[...] = along_y.reshape(out_a.shape).astype(jnp.bfloat16)

    def exchange_a():
        def send(k, carry):
            d, l = peer(k)
            pltpu.make_async_remote_copy(
                out_a.at[l * depths + d], in_a.at[depth, lat], send_a, recv_a,
                device_id=(d, l), device_id_type=MESH,
            ).start()
            return carry

        pltpu.make_async_copy(out_a.at[lat * depths + depth], in_a.at[depth, lat], recv_a).start()
        lax.fori_loop(1, devices, send, 0)

    def exchange_b():
        def send(k, carry):
            d, l = peer(k)
            pltpu.make_async_remote_copy(
                out_b.at[d, l], in_b.at[lat * depths + depth], send_b, recv_b,
                device_id=(d, l), device_id_type=MESH,
            ).start()
            return carry

        pltpu.make_async_copy(out_b.at[depth, lat], in_b.at[lat * depths + depth], recv_b).start()
        lax.fori_loop(1, devices, send, 0)

    def slab_copy(k):
        d = lax.rem(depth + k, depths)
        return pltpu.make_async_remote_copy(
            green.at[0, :, :, pl.ds(pl.multiple_of(d * rows, rows), rows)],
            slabs.at[depth], slab_send.at[d], slab_recv.at[depth],
            device_id=(d, lat), device_id_type=MESH,
        )

    field = incident[...].reshape(sources_count * 2 * part, length)
    for iteration in range(ITERS):
        spread_along_y(field)
        if iteration == 0:
            pl.semaphore_wait(barrier, devices - 1)
        exchange_a()
        if iteration == 0:
            def deal(k, carry):
                slab_copy(k).start()
                return carry

            lax.fori_loop(1, depths, deal, 0)
        pltpu.make_async_copy(in_a, in_a, recv_a).wait()
        blocks = [
            in_a[:, l].astype(jnp.float32).reshape(depths * rows, sources_count * lanes)
            for l in range(lats)
        ]
        for s in range(sources_count):
            half = jnp.concatenate(
                [b[:, s * lanes:(s + 1) * lanes] for b in blocks], axis=1
            ).astype(jnp.bfloat16)
            spectra[s] = jnp.dot(
                half, forward_x[...], preferred_element_type=jnp.float32
            ).reshape(depths, rows, 2 * period)

        def couple(k, carry):
            z = lax.rem(depth + k, depths)
            if iteration == 0:
                pltpu.make_async_copy(slabs.at[z], slabs.at[z], slab_recv.at[z]).wait()
            reals = [jnp.zeros((rows, period), jnp.float32) for _ in range(sources_count)]
            imags = [jnp.zeros((rows, period), jnp.float32) for _ in range(sources_count)]
            for w in range(depths):
                kern_real = slabs[z, w, 0].astype(jnp.float32)
                kern_imag = slabs[z, w, 1].astype(jnp.float32)
                for s in range(sources_count):
                    spec_real = spectra[s, w, :, :period]
                    spec_imag = spectra[s, w, :, period:]
                    reals[s] += kern_real * spec_real - kern_imag * spec_imag
                    imags[s] += kern_real * spec_imag + kern_imag * spec_real
            for s in range(sources_count):
                scattered[s, z, :, :period] = reals[s]
                scattered[s, z, :, period:] = imags[s]
            return carry

        lax.fori_loop(0, depths, couple, 0)
        returned = [
            jnp.dot(
                scattered[s].reshape(depths * rows, 2 * period).astype(jnp.bfloat16),
                inverse_x[...],
                preferred_element_type=jnp.float32,
            )
            for s in range(sources_count)
        ]
        pltpu.make_async_copy(out_a.at[1:], out_a.at[1:], send_a).wait()
        for l in range(lats):
            out_b[:, l] = jnp.concatenate(
                [r[:, l * lanes:(l + 1) * lanes] for r in returned], axis=1
            ).reshape(depths, rows, sources_count * lanes).astype(jnp.bfloat16)
        exchange_b()
        pltpu.make_async_copy(in_b, in_b, recv_b).wait()
        along_x = in_b[...].astype(jnp.float32).reshape(period, sources_count * lanes).astype(jnp.bfloat16)
        turned = lax.dot_general(
            along_x, inverse_y[...], (((0,), (0,)), ((), ())), preferred_element_type=jnp.float32
        )
        cosine = halves(turned[:, :length])
        sine = halves(turned[:, length:])
        sums = jnp.concatenate(
            [cosine[:, 0:1] - sine[:, 1:2], cosine[:, 1:2] + sine[:, 0:1]], axis=1
        )
        field = (incident[0] + sums * (1.0 / float(period * period))).reshape(field.shape)
        slots = out_b.reshape(devices, rows, sources_count * lanes)
        pltpu.make_async_copy(slots.at[1:], slots.at[1:], send_b).wait()
    out[...] = field.reshape(out.shape)

    def sent(k, carry):
        slab_copy(k).wait_send()
        return carry

    lax.fori_loop(1, depths, sent, 0)


def born(depths, lats, incident, contrast, kernel):
    sources_count, part, length = incident.shape[1], incident.shape[3], incident.shape[4]
    devices = depths * lats
    period = 2 * length
    rows = period // devices
    lanes = sources_count * 2 * part
    vmem = pl.BlockSpec(memory_space=pltpu.VMEM)
    block = jnp.bfloat16
    return pl.pallas_call(
        functools.partial(born_kernel, depths, lats),
        out_shape=jax.ShapeDtypeStruct(incident.shape, jnp.float32),
        in_specs=[vmem, vmem, pl.BlockSpec(memory_space=pl.ANY)] + [vmem] * 4,
        out_specs=vmem,
        scratch_shapes=[
            pltpu.VMEM((depths, depths, 2, rows, period), block),
            pltpu.VMEM((devices, rows, lanes), block),
            pltpu.VMEM((depths, lats, rows, lanes), block),
            pltpu.VMEM((depths, lats, rows, lanes), block),
            pltpu.VMEM((devices, rows, lanes), block),
            pltpu.VMEM((sources_count, depths, rows, 2 * period), jnp.float32),
            pltpu.VMEM((sources_count, depths, rows, 2 * period), jnp.float32),
            pltpu.SemaphoreType.DMA((depths,)),
            pltpu.SemaphoreType.DMA((depths,)),
            pltpu.SemaphoreType.DMA,
            pltpu.SemaphoreType.DMA,
            pltpu.SemaphoreType.DMA,
            pltpu.SemaphoreType.DMA,
        ],
        compiler_params=pltpu.CompilerParams(collective_id=0, has_side_effects=True),
        name="born",
    )(incident, contrast, kernel, *tables(length, lats))


def solution(mesh):
    in_specs = (
        P("depth", None, None, "lat", None),
        P("depth", "lat", None),
        P("depth", None, None, "lat", None),
    )
    out_specs = P("depth", None, None, "lat", None)
    depths, lats = mesh.shape["depth"], mesh.shape["lat"]

    def run(incident, contrast, kernel):
        if (2 * incident.shape[4]) % (8 * depths * lats) == 0:
            return born(depths, lats, incident, contrast, kernel)
        return local(incident, contrast, kernel)

    return jax.shard_map(run, mesh=mesh, in_specs=in_specs, out_specs=out_specs, check_vma=False)
```

```python
import functools
import math

import jax
import jax.numpy as jnp
import numpy as np
from jax import lax
from jax.experimental import pallas as pl
from jax.experimental.pallas import tpu as pltpu
from jax.sharding import PartitionSpec as P

ITERS = 3
GROUP = 4
MESH = pl.DeviceIdType.MESH


def dft(rows, columns, period):
    angles = (np.outer(np.arange(rows), np.arange(columns)) % period) * (2.0 * math.pi / period)
    return np.cos(angles), np.sin(angles)


def tables(length, lats):
    period = 2 * length
    part = length // lats
    cos_f, sin_f = dft(length, period, period)
    cos_i, sin_i = dft(period, length, period)
    forward_y = np.concatenate([cos_f.T, sin_f.T], axis=1)
    inverse_y = np.concatenate([cos_i, sin_i], axis=1)
    real_rows = np.concatenate([cos_f, -sin_f], axis=1).reshape(lats, part, 2 * period)
    imag_rows = np.concatenate([sin_f, cos_f], axis=1).reshape(lats, part, 2 * period)
    forward_x = np.stack([real_rows, imag_rows], axis=1).reshape(2 * length, 2 * period)
    to_real = np.concatenate([cos_i, -sin_i], axis=0).reshape(2 * period, lats, part)
    to_imag = np.concatenate([sin_i, cos_i], axis=0).reshape(2 * period, lats, part)
    inverse_x = np.stack([to_real, to_imag], axis=2).reshape(2 * period, 2 * length)
    return tuple(jnp.asarray(t, jnp.bfloat16) for t in (forward_y, forward_x, inverse_x, inverse_y))


def born_kernel(
    depths, lats, group,
    incident, contrast, green, forward_y, forward_x, inverse_x, inverse_y, out,
    slabs, out_a, in_a, out_b, in_b, spectra, scattered,
    slab_send, slab_recv, send_a, recv_a, send_b, recv_b,
):
    depth = lax.axis_index("depth")
    lat = lax.axis_index("lat")
    devices = depths * lats
    me = depth * lats + lat
    place = lax.rem(depth, group)
    first = depth - place
    rows = out_a.shape[1]
    sources_count, _, part, length = incident.shape[1:]
    lanes = 2 * part
    period = inverse_y.shape[0]

    def peer(k):
        number = lax.rem(me + k, devices)
        return number // lats, lax.rem(number, lats)

    def member(k):
        number = lax.rem(place * lats + lat + k, group * lats)
        return number // lats, lax.rem(number, lats)

    barrier = pltpu.get_barrier_semaphore()

    def greet(k, carry):
        pl.semaphore_signal(barrier, inc=1, device_id=peer(k), device_id_type=MESH)
        return carry

    lax.fori_loop(1, devices, greet, 0)

    own = pltpu.make_async_copy(
        green.at[0, :, :, pl.ds(pl.multiple_of(place * rows, rows), rows)],
        slabs.at[place],
        slab_recv.at[place],
    )
    own.start()

    def halves(field):
        return field.reshape(sources_count, 2, part, length)

    def spread_along_y(field):
        driven = contrast[0][None, None] * halves(field)
        turned = jnp.concatenate([driven[:, 1:2], -driven[:, 0:1]], axis=1)
        flat = (sources_count * 2 * part, length)
        both = jnp.concatenate([driven.reshape(flat), turned.reshape(flat)], axis=1).astype(jnp.bfloat16)
        along_y = lax.dot_general(
            forward_y[...], both, (((1,), (1,)), ((), ())), preferred_element_type=jnp.float32
        )
        out_a[...] = along_y.reshape(out_a.shape).astype(jnp.bfloat16)

    def exchange_a(slot):
        def send(k, carry):
            d, l = peer(k)
            pltpu.make_async_remote_copy(
                out_a.at[l * group + lax.rem(d, group)], in_a.at[slot, depth, lat], send_a, recv_a.at[slot],
                device_id=(d, l), device_id_type=MESH,
            ).start()
            return carry

        pltpu.make_async_copy(out_a.at[lat * group + place], in_a.at[slot, depth, lat], recv_a.at[slot]).start()
        lax.fori_loop(1, devices, send, 0)

    def exchange_b():
        def send(k, carry):
            d, l = member(k)
            pltpu.make_async_remote_copy(
                out_b.at[d, l], in_b.at[lat * group + place], send_b, recv_b,
                device_id=(first + d, l), device_id_type=MESH,
            ).start()
            return carry

        pltpu.make_async_copy(out_b.at[place, lat], in_b.at[lat * group + place], recv_b).start()
        lax.fori_loop(1, group * lats, send, 0)

    def slab_copy(k):
        d = lax.rem(place + k, group)
        return pltpu.make_async_remote_copy(
            green.at[0, :, :, pl.ds(pl.multiple_of(d * rows, rows), rows)],
            slabs.at[place], slab_send.at[d], slab_recv.at[place],
            device_id=(first + d, lat), device_id_type=MESH,
        )

    field = incident[...].reshape(sources_count * 2 * part, length)
    for iteration in range(ITERS):
        spread_along_y(field)
        if iteration == 0:
            pl.semaphore_wait(barrier, devices - 1)
        slot = iteration % 2
        exchange_a(slot)
        if iteration == 0:
            def deal(k, carry):
                slab_copy(k).start()
                return carry

            lax.fori_loop(1, group, deal, 0)
        pltpu.make_async_copy(in_a.at[slot], in_a.at[slot], recv_a.at[slot]).wait()
        blocks = [
            in_a[slot, :, l].astype(jnp.float32).reshape(depths * rows, sources_count * lanes)
            for l in range(lats)
        ]
        for s in range(sources_count):
            half = jnp.concatenate(
                [b[:, s * lanes:(s + 1) * lanes] for b in blocks], axis=1
            ).astype(jnp.bfloat16)
            spectra[s] = jnp.dot(
                half, forward_x[...], preferred_element_type=jnp.float32
            ).reshape(depths, rows, 2 * period)

        def couple(k, carry):
            z = lax.rem(place + k, group)
            if iteration == 0:
                pltpu.make_async_copy(slabs.at[z], slabs.at[z], slab_recv.at[z]).wait()
            zero = jnp.zeros((rows, period), jnp.float32)

            def add(w, sums):
                kern_real = slabs[z, w, 0].astype(jnp.float32)
                kern_imag = slabs[z, w, 1].astype(jnp.float32)
                new = []
                for s in range(sources_count):
                    spec_real = spectra[s, w, :, :period]
                    spec_imag = spectra[s, w, :, period:]
                    new.append(sums[2 * s] + (kern_real * spec_real - kern_imag * spec_imag))
                    new.append(sums[2 * s + 1] + (kern_real * spec_imag + kern_imag * spec_real))
                return tuple(new)

            sums = lax.fori_loop(0, depths, add, (zero,) * (2 * sources_count), unroll=4)
            for s in range(sources_count):
                scattered[s, z, :, :period] = sums[2 * s]
                scattered[s, z, :, period:] = sums[2 * s + 1]
            return carry

        lax.fori_loop(0, group, couple, 0)
        returned = [
            jnp.dot(
                scattered[s].reshape(group * rows, 2 * period).astype(jnp.bfloat16),
                inverse_x[...],
                preferred_element_type=jnp.float32,
            )
            for s in range(sources_count)
        ]
        flat_a = in_a.at[slot].reshape(devices, rows, sources_count * lanes)
        pltpu.make_async_copy(flat_a.at[1:], flat_a.at[1:], send_a).wait()
        for l in range(lats):
            out_b[:, l] = jnp.concatenate(
                [r[:, l * lanes:(l + 1) * lanes] for r in returned], axis=1
            ).reshape(group, rows, sources_count * lanes).astype(jnp.bfloat16)
        exchange_b()
        pltpu.make_async_copy(in_b, in_b, recv_b).wait()
        along_x = in_b[...].astype(jnp.float32).reshape(period, sources_count * lanes).astype(jnp.bfloat16)
        turned = lax.dot_general(
            along_x, inverse_y[...], (((0,), (0,)), ((), ())), preferred_element_type=jnp.float32
        )
        cosine = halves(turned[:, :length])
        sine = halves(turned[:, length:])
        sums = jnp.concatenate(
            [cosine[:, 0:1] - sine[:, 1:2], cosine[:, 1:2] + sine[:, 0:1]], axis=1
        )
        field = (incident[0] + sums * (1.0 / float(period * period))).reshape(field.shape)
        pltpu.make_async_copy(in_b.at[1:], in_b.at[1:], send_b).wait()
    out[...] = field.reshape(out.shape)

    def sent(k, carry):
        slab_copy(k).wait_send()
        return carry

    lax.fori_loop(1, group, sent, 0)


def born(depths, lats, incident, contrast, kernel):
    sources_count, part, length = incident.shape[1], incident.shape[3], incident.shape[4]
    period = 2 * length
    group = math.gcd(GROUP, depths)
    rows = period // (group * lats)
    lanes = sources_count * 2 * part
    vmem = pl.BlockSpec(memory_space=pltpu.VMEM)
    block = jnp.bfloat16
    return pl.pallas_call(
        functools.partial(born_kernel, depths, lats, group),
        out_shape=jax.ShapeDtypeStruct(incident.shape, jnp.float32),
        in_specs=[vmem, vmem, pl.BlockSpec(memory_space=pl.ANY)] + [vmem] * 4,
        out_specs=vmem,
        scratch_shapes=[
            pltpu.VMEM((group, depths, 2, rows, period), block),
            pltpu.VMEM((group * lats, rows, lanes), block),
            pltpu.VMEM((2, depths, lats, rows, lanes), block),
            pltpu.VMEM((group, lats, rows, lanes), block),
            pltpu.VMEM((group * lats, rows, lanes), block),
            pltpu.VMEM((sources_count, depths, rows, 2 * period), jnp.float32),
            pltpu.VMEM((sources_count, group, rows, 2 * period), jnp.float32),
            pltpu.SemaphoreType.DMA((group,)),
            pltpu.SemaphoreType.DMA((group,)),
            pltpu.SemaphoreType.DMA,
            pltpu.SemaphoreType.DMA((2,)),
            pltpu.SemaphoreType.DMA,
            pltpu.SemaphoreType.DMA,
        ],
        compiler_params=pltpu.CompilerParams(collective_id=0, has_side_effects=True),
        name="born",
    )(incident, contrast, kernel, *tables(length, lats))


def solution(mesh):
    in_specs = (
        P("depth", None, None, "lat", None),
        P("depth", "lat", None),
        P("depth", None, None, "lat", None),
    )
    out_specs = P("depth", None, None, "lat", None)
    run = functools.partial(born, mesh.shape["depth"], mesh.shape["lat"])
    return jax.shard_map(run, mesh=mesh, in_specs=in_specs, out_specs=out_specs, check_vma=False)
```

```python
import functools
import math

import jax
import jax.numpy as jnp
import numpy as np
from jax import lax
from jax.experimental import pallas as pl
from jax.experimental.pallas import tpu as pltpu
from jax.sharding import PartitionSpec as P

ITERS = 3
GROUP = 4
MESH = pl.DeviceIdType.MESH


def dft(rows, columns, period):
    angles = (np.outer(np.arange(rows), np.arange(columns)) % period) * (2.0 * math.pi / period)
    return np.cos(angles), np.sin(angles)


def tables(length, lats):
    period = 2 * length
    part = length // lats
    cos_f, sin_f = dft(length, period, period)
    cos_i, sin_i = dft(period, length, period)
    waves_y = np.concatenate([cos_i, sin_i], axis=1)
    real_rows = np.concatenate([cos_f, -sin_f], axis=1).reshape(lats, part, 2 * period)
    imag_rows = np.concatenate([sin_f, cos_f], axis=1).reshape(lats, part, 2 * period)
    forward_x = np.stack([real_rows, imag_rows], axis=1).reshape(2 * length, 2 * period)
    to_real = np.concatenate([cos_i, -sin_i], axis=0).reshape(2 * period, lats, part)
    to_imag = np.concatenate([sin_i, cos_i], axis=0).reshape(2 * period, lats, part)
    inverse_x = np.stack([to_real, to_imag], axis=2).reshape(2 * period, 2 * length)
    return tuple(jnp.asarray(t, jnp.bfloat16) for t in (waves_y, forward_x, inverse_x))


def born_kernel(
    depths, lats, group,
    incident_hbm, contrast_hbm, green, waves_y_hbm, forward_x_hbm, inverse_x_hbm, out,
    incident, contrast, waves_y, forward_x, inverse_x,
    slabs, out_a, in_a, out_b, in_b, spectra, scattered,
    loads, slab_send, slab_recv, send_a, recv_a, send_b, recv_b,
):
    depth = lax.axis_index("depth")
    lat = lax.axis_index("lat")
    devices = depths * lats
    members = group * lats
    me = depth * lats + lat
    place = lax.rem(depth, group)
    first = depth - place
    half = out_a.shape[2]
    rows = 2 * half
    sources_count, _, part, length = incident.shape[1:]
    lanes = 2 * part
    period = 2 * length

    def peer(k):
        number = lax.rem(me + k, devices)
        return number // lats, lax.rem(number, lats)

    def member(k):
        number = lax.rem(place * lats + lat + k, members)
        return number // lats, lax.rem(number, lats)

    barrier = pltpu.get_barrier_semaphore()

    def greet(k, carry):
        pl.semaphore_signal(barrier, inc=1, device_id=peer(k), device_id_type=MESH)
        return carry

    lax.fori_loop(1, devices, greet, 0)

    pairs = (
        (contrast_hbm, contrast), (incident_hbm, incident), (waves_y_hbm, waves_y),
        (forward_x_hbm, forward_x), (inverse_x_hbm, inverse_x),
    )
    copies = [pltpu.make_async_copy(a, b, loads.at[n]) for n, (a, b) in enumerate(pairs)]
    own = pltpu.make_async_copy(
        green.at[0, :, :, pl.ds(pl.multiple_of(place * rows, rows), rows)],
        slabs.at[place],
        slab_recv.at[place],
    )
    for copy in copies:
        copy.start()
    own.start()

    def spread_along_y(s, field):
        driven = contrast[0][None] * field.reshape(2, part, length)
        turned = jnp.concatenate([driven[1:2], -driven[0:1]], axis=0)
        both = jnp.concatenate(
            [driven.reshape(lanes, length), turned.reshape(lanes, length)], axis=1
        ).astype(jnp.bfloat16)
        along_y = lax.dot_general(
            waves_y[...], both, (((1,), (1,)), ((), ())), preferred_element_type=jnp.float32
        ).reshape(members, 2, half, lanes)
        out_a[s] = jnp.concatenate([along_y[:, 0], along_y[:, 1]], axis=-1).astype(jnp.bfloat16)

    def exchange_a(slot, s):
        def start(d, l):
            pltpu.make_async_remote_copy(
                out_a.at[s, l * group + lax.rem(d, group)], in_a.at[slot, s, depth, lat],
                send_a.at[s], recv_a.at[slot, s],
                device_id=(d, l), device_id_type=MESH,
            ).start()

        def far(k, carry):
            d, l = member(lax.rem(k, members))
            start(lax.rem(first + (k // members + 1) * group, depths) + d, l)
            return carry

        def near(k, carry):
            d, l = member(k)
            start(first + d, l)
            return carry

        lax.fori_loop(0, devices - members, far, 0, unroll=members)
        lax.fori_loop(1, members, near, 0, unroll=True)
        pltpu.make_async_copy(
            out_a.at[s, lat * group + place], in_a.at[slot, s, depth, lat], recv_a.at[slot, s]
        ).start()

    def sent_a(s):
        block = in_a.at[0, s].reshape(devices, half, 2 * lanes).at[1:]
        pltpu.make_async_copy(block, block, send_a.at[s]).wait()

    def exchange_b(s):
        def send(k, carry):
            d, l = member(k)
            pltpu.make_async_remote_copy(
                out_b.at[s, d, l], in_b.at[s, lat * group + place], send_b.at[s], recv_b.at[s],
                device_id=(first + d, l), device_id_type=MESH,
            ).start()
            return carry

        lax.fori_loop(1, members, send, 0, unroll=True)
        pltpu.make_async_copy(
            out_b.at[s, place, lat], in_b.at[s, lat * group + place], recv_b.at[s]
        ).start()

    def sent_b(s):
        block = in_b.at[s, 1:]
        pltpu.make_async_copy(block, block, send_b.at[s]).wait()

    def slab_copy(k):
        d = lax.rem(place + k, group)
        return pltpu.make_async_remote_copy(
            green.at[0, :, :, pl.ds(pl.multiple_of(d * rows, rows), rows)],
            slabs.at[place], slab_send.at[d], slab_recv.at[place],
            device_id=(first + d, lat), device_id_type=MESH,
        )

    def couple(s, wait_slabs):
        zero = jnp.zeros((rows, period), jnp.float32)

        def receive(k, carry):
            z = lax.rem(place + k, group)
            if wait_slabs:
                pltpu.make_async_copy(slabs.at[z], slabs.at[z], slab_recv.at[z]).wait()

            def add(w, sums):
                kern_real = slabs[z, w, 0].astype(jnp.float32)
                kern_imag = slabs[z, w, 1].astype(jnp.float32)
                spec_real = spectra[w, :, :period]
                spec_imag = spectra[w, :, period:]
                return (
                    sums[0] + (kern_real * spec_real - kern_imag * spec_imag),
                    sums[1] + (kern_real * spec_imag + kern_imag * spec_real),
                )

            real, imag = lax.fori_loop(0, depths, add, (zero, zero), unroll=8)
            scattered[z, :, :period] = real
            scattered[z, :, period:] = imag
            return carry

        lax.fori_loop(0, group, receive, 0)

    def scatter(iteration, slot, s):
        pltpu.make_async_copy(in_a.at[slot, s], in_a.at[slot, s], recv_a.at[slot, s]).wait()
        blocks = [
            in_a[slot, s, :, l].astype(jnp.float32).reshape(depths * half, 2 * lanes)
            for l in range(lats)
        ]
        for h in range(2):
            along_y = jnp.concatenate(
                [b[:, h * lanes:(h + 1) * lanes] for b in blocks], axis=1
            ).astype(jnp.bfloat16)
            spectra[:, h * half:(h + 1) * half] = jnp.dot(
                along_y, forward_x[...], preferred_element_type=jnp.float32
            ).reshape(depths, half, 2 * period)
        couple(s, iteration == 0 and s == 0)
        along_x = jnp.dot(
            scattered[...].reshape(group * rows, 2 * period).astype(jnp.bfloat16),
            inverse_x[...],
            preferred_element_type=jnp.float32,
        )
        if iteration > 0:
            sent_b(s)
        for l in range(lats):
            mine = along_x[:, l * lanes:(l + 1) * lanes].reshape(group, 2, half, lanes)
            out_b[s, :, l] = jnp.concatenate([mine[:, 0], mine[:, 1]], axis=-1).astype(jnp.bfloat16)

    def gather_field(s):
        pltpu.make_async_copy(in_b.at[s], in_b.at[s], recv_b.at[s]).wait()
        blocks = in_b[s].astype(jnp.float32)
        along_x = jnp.stack(
            [blocks[:, :, :lanes], blocks[:, :, lanes:]], axis=1
        ).reshape(period, lanes).astype(jnp.bfloat16)
        turned = lax.dot_general(
            along_x, waves_y[...], (((0,), (0,)), ((), ())), preferred_element_type=jnp.float32
        )
        cosine = turned[:, :length].reshape(2, part, length)
        sine = turned[:, length:].reshape(2, part, length)
        sums = jnp.concatenate([cosine[0:1] - sine[1:2], cosine[1:2] + sine[0:1]], axis=0)
        return incident[0, s] + sums * (1.0 / float(period * period))

    for iteration in range(ITERS):
        slot = iteration % 2
        for s in range(sources_count):
            if iteration == 0:
                if s == 0:
                    for copy in copies[:3]:
                        copy.wait()
                field = incident[0, s]
            else:
                field = gather_field(s)
                sent_a(s)
            spread_along_y(s, field)
            if iteration > 0:
                exchange_a(slot, s)
        if iteration == 0:
            pl.semaphore_wait(barrier, devices - 1)
            for s in range(sources_count):
                exchange_a(slot, s)

            def deal(k, carry):
                slab_copy(k).start()
                return carry

            lax.fori_loop(1, group, deal, 0)
            for copy in copies[3:]:
                copy.wait()
        for s in range(sources_count):
            scatter(iteration, slot, s)
            exchange_b(s)
    for s in range(sources_count):
        out[0, s] = gather_field(s)
        sent_a(s)
        sent_b(s)

    def sent(k, carry):
        slab_copy(k).wait_send()
        return carry

    lax.fori_loop(1, group, sent, 0)


def born(depths, lats, incident, contrast, kernel):
    sources_count, part, length = incident.shape[1], incident.shape[3], incident.shape[4]
    period = 2 * length
    group = math.gcd(GROUP, depths)
    rows = period // (group * lats)
    half = rows // 2
    lanes = 4 * part
    block = jnp.bfloat16
    waves_y, forward_x, inverse_x = tables(length, lats)
    held = (incident, contrast, waves_y, forward_x, inverse_x)
    anywhere = pl.BlockSpec(memory_space=pl.ANY)
    return pl.pallas_call(
        functools.partial(born_kernel, depths, lats, group),
        out_shape=pltpu.VMEM(incident.shape, jnp.float32),
        in_specs=[anywhere] * 6,
        out_specs=pl.BlockSpec(memory_space=pltpu.VMEM),
        scratch_shapes=[pltpu.VMEM(a.shape, a.dtype) for a in held] + [
            pltpu.VMEM((group, depths, 2, rows, period), block),
            pltpu.VMEM((sources_count, group * lats, half, lanes), block),
            pltpu.VMEM((2, sources_count, depths, lats, half, lanes), block),
            pltpu.VMEM((sources_count, group, lats, half, lanes), block),
            pltpu.VMEM((sources_count, group * lats, half, lanes), block),
            pltpu.VMEM((depths, rows, 2 * period), jnp.float32),
            pltpu.VMEM((group, rows, 2 * period), jnp.float32),
            pltpu.SemaphoreType.DMA((len(held),)),
            pltpu.SemaphoreType.DMA((group,)),
            pltpu.SemaphoreType.DMA((group,)),
            pltpu.SemaphoreType.DMA((sources_count,)),
            pltpu.SemaphoreType.DMA((2, sources_count)),
            pltpu.SemaphoreType.DMA((sources_count,)),
            pltpu.SemaphoreType.DMA((sources_count,)),
        ],
        compiler_params=pltpu.CompilerParams(collective_id=0, has_side_effects=True),
        name="born",
    )(incident, contrast, kernel, waves_y, forward_x, inverse_x)


def solution(mesh):
    in_specs = (
        P("depth", None, None, "lat", None),
        P("depth", "lat", None),
        P("depth", None, None, "lat", None),
    )
    out_specs = P("depth", None, None, "lat", None)
    run = functools.partial(born, mesh.shape["depth"], mesh.shape["lat"])
    return jax.shard_map(run, mesh=mesh, in_specs=in_specs, out_specs=out_specs, check_vma=False)
```

```python
import functools
import math

import jax
import jax.numpy as jnp
import numpy as np
from jax import lax
from jax.experimental import pallas as pl
from jax.experimental.pallas import tpu as pltpu
from jax.sharding import PartitionSpec as P

ITERS = 3
GROUP = 4
MESH = pl.DeviceIdType.MESH


def dft(rows, columns, period):
    angles = (np.outer(np.arange(rows), np.arange(columns)) % period) * (2.0 * math.pi / period)
    return np.cos(angles), np.sin(angles)


def tables(length, lats):
    period = 2 * length
    part = length // lats
    cos_f, sin_f = dft(length, period, period)
    cos_i, sin_i = dft(period, length, period)
    waves_y = np.concatenate([cos_i, sin_i], axis=1)
    real_rows = np.concatenate([cos_f, -sin_f], axis=1).reshape(lats, part, 2 * period)
    imag_rows = np.concatenate([sin_f, cos_f], axis=1).reshape(lats, part, 2 * period)
    forward_x = np.stack([real_rows, imag_rows], axis=1).reshape(2 * length, 2 * period)
    to_real = np.concatenate([cos_i, -sin_i], axis=0).reshape(2 * period, lats, part)
    to_imag = np.concatenate([sin_i, cos_i], axis=0).reshape(2 * period, lats, part)
    inverse_x = np.stack([to_real, to_imag], axis=2).reshape(2 * period, 2 * length)
    return tuple(jnp.asarray(t, jnp.bfloat16) for t in (waves_y, forward_x, inverse_x))


def born_kernel(
    depths, lats, group,
    incident_hbm, contrast_hbm, green, waves_y_hbm, forward_x_hbm, inverse_x_hbm, out,
    incident, contrast, waves_y, forward_x, inverse_x,
    slabs, out_a, in_a, out_b, in_b, spectra, scattered,
    loads, slab_send, slab_recv, send_a, recv_a, send_b, recv_b,
):
    depth = lax.axis_index("depth")
    lat = lax.axis_index("lat")
    devices = depths * lats
    members = group * lats
    me = depth * lats + lat
    place = lax.rem(depth, group)
    first = depth - place
    half = out_a.shape[2]
    rows = 2 * half
    sources_count, _, part, length = incident.shape[1:]
    lanes = 2 * part
    period = 2 * length

    def peer(k):
        number = lax.rem(me + k, devices)
        return number // lats, lax.rem(number, lats)

    def member(k):
        number = lax.rem(place * lats + lat + k, members)
        return number // lats, lax.rem(number, lats)

    barrier = pltpu.get_barrier_semaphore()

    def greet(k, carry):
        pl.semaphore_signal(barrier, inc=1, device_id=peer(k), device_id_type=MESH)
        return carry

    lax.fori_loop(1, devices, greet, 0)

    pairs = (
        (contrast_hbm, contrast), (incident_hbm, incident), (waves_y_hbm, waves_y),
        (forward_x_hbm, forward_x), (inverse_x_hbm, inverse_x),
    )
    copies = [pltpu.make_async_copy(a, b, loads.at[n]) for n, (a, b) in enumerate(pairs)]
    own = pltpu.make_async_copy(
        green.at[0, :, :, pl.ds(pl.multiple_of(place * rows, rows), rows)],
        slabs.at[place],
        slab_recv.at[place],
    )
    for copy in copies:
        copy.start()
    own.start()

    def spread_along_y(s, field):
        driven = contrast[0][None] * field.reshape(2, part, length)
        turned = jnp.concatenate([driven[1:2], -driven[0:1]], axis=0)
        both = jnp.concatenate(
            [driven.reshape(lanes, length), turned.reshape(lanes, length)], axis=1
        ).astype(jnp.bfloat16)
        along_y = lax.dot_general(
            waves_y[...], both, (((1,), (1,)), ((), ())), preferred_element_type=jnp.float32
        ).reshape(members, 2, half, lanes)
        out_a[s] = jnp.concatenate([along_y[:, 0], along_y[:, 1]], axis=-1).astype(jnp.bfloat16)

    def exchange_a(slot, s):
        def start(d, l):
            pltpu.make_async_remote_copy(
                out_a.at[s, l * group + lax.rem(d, group)], in_a.at[slot, s, depth, lat],
                send_a.at[s], recv_a.at[slot, s],
                device_id=(d, l), device_id_type=MESH,
            ).start()

        def far(k, carry):
            d, l = member(lax.rem(k, members))
            start(lax.rem(first + (k // members + 1) * group, depths) + d, l)
            return carry

        def near(k, carry):
            d, l = member(k)
            start(first + d, l)
            return carry

        lax.fori_loop(0, devices - members, far, 0, unroll=members)
        lax.fori_loop(1, members, near, 0, unroll=True)
        pltpu.make_async_copy(
            out_a.at[s, lat * group + place], in_a.at[slot, s, depth, lat], recv_a.at[slot, s]
        ).start()

    def sent_a(s):
        block = in_a.at[0, s].reshape(devices, half, 2 * lanes).at[1:]
        pltpu.make_async_copy(block, block, send_a.at[s]).wait()

    def exchange_b(s):
        def send(k, carry):
            d, l = member(k)
            pltpu.make_async_remote_copy(
                out_b.at[s, d, l], in_b.at[s, lat * group + place], send_b.at[s], recv_b.at[s],
                device_id=(first + d, l), device_id_type=MESH,
            ).start()
            return carry

        lax.fori_loop(1, members, send, 0, unroll=True)
        pltpu.make_async_copy(
            out_b.at[s, place, lat], in_b.at[s, lat * group + place], recv_b.at[s]
        ).start()

    def sent_b(s):
        block = in_b.at[s, 1:]
        pltpu.make_async_copy(block, block, send_b.at[s]).wait()

    def slab_copy(k):
        d = lax.rem(place + k, group)
        return pltpu.make_async_remote_copy(
            green.at[0, :, :, pl.ds(pl.multiple_of(d * rows, rows), rows)],
            slabs.at[place], slab_send.at[d], slab_recv.at[place],
            device_id=(first + d, lat), device_id_type=MESH,
        )

    def couple(s, wait_slabs):
        zero = jnp.zeros((rows, period), jnp.float32)

        def receive(k, carry):
            z = lax.rem(place + k, group)
            if wait_slabs:
                pltpu.make_async_copy(slabs.at[z], slabs.at[z], slab_recv.at[z]).wait()

            def add(w, sums):
                kern_real = slabs[z, w, 0].astype(jnp.float32)
                kern_imag = slabs[z, w, 1].astype(jnp.float32)
                spec_real = spectra[w, :, :period]
                spec_imag = spectra[w, :, period:]
                return (
                    sums[0] + (kern_real * spec_real - kern_imag * spec_imag),
                    sums[1] + (kern_real * spec_imag + kern_imag * spec_real),
                )

            real, imag = lax.fori_loop(0, depths, add, (zero, zero), unroll=8)
            scattered[z, :, :period] = real
            scattered[z, :, period:] = imag
            return carry

        lax.fori_loop(0, group, receive, 0)

    def scatter(iteration, slot, s):
        pltpu.make_async_copy(in_a.at[slot, s], in_a.at[slot, s], recv_a.at[slot, s]).wait()
        blocks = [
            in_a[slot, s, :, l].astype(jnp.float32).reshape(depths * half, 2 * lanes)
            for l in range(lats)
        ]
        for h in range(2):
            along_y = jnp.concatenate(
                [b[:, h * lanes:(h + 1) * lanes] for b in blocks], axis=1
            ).astype(jnp.bfloat16)
            spectra[:, h * half:(h + 1) * half] = jnp.dot(
                along_y, forward_x[...], preferred_element_type=jnp.float32
            ).reshape(depths, half, 2 * period)
        couple(s, iteration == 0 and s == 0)
        along_x = jnp.dot(
            scattered[...].reshape(group * rows, 2 * period).astype(jnp.bfloat16),
            inverse_x[...],
            preferred_element_type=jnp.float32,
        )
        if iteration > 0:
            sent_b(s)
        for l in range(lats):
            mine = along_x[:, l * lanes:(l + 1) * lanes].reshape(group, 2, half, lanes)
            out_b[s, :, l] = jnp.concatenate([mine[:, 0], mine[:, 1]], axis=-1).astype(jnp.bfloat16)

    def gather_field(s):
        pltpu.make_async_copy(in_b.at[s], in_b.at[s], recv_b.at[s]).wait()
        blocks = in_b[s].astype(jnp.float32)
        along_x = jnp.stack(
            [blocks[:, :, :lanes], blocks[:, :, lanes:]], axis=1
        ).reshape(period, lanes).astype(jnp.bfloat16)
        turned = lax.dot_general(
            along_x, waves_y[...], (((0,), (0,)), ((), ())), preferred_element_type=jnp.float32
        )
        cosine = turned[:, :length].reshape(2, part, length)
        sine = turned[:, length:].reshape(2, part, length)
        sums = jnp.concatenate([cosine[0:1] - sine[1:2], cosine[1:2] + sine[0:1]], axis=0)
        return incident[0, s] + sums * (1.0 / float(period * period))

    for iteration in range(ITERS):
        slot = iteration % 2
        for s in range(sources_count):
            if iteration == 0:
                if s == 0:
                    for copy in copies[:3]:
                        copy.wait()
                field = incident[0, s]
            else:
                field = gather_field(s)
                sent_a(s)
            spread_along_y(s, field)
            if iteration > 0:
                exchange_a(slot, s)
        if iteration == 0:
            pl.semaphore_wait(barrier, devices - 1)
            def deal(k, carry):
                slab_copy(k).start()
                return carry

            for s in range(sources_count):
                exchange_a(slot, s)
                if s == 0:
                    lax.fori_loop(1, group, deal, 0)

            for copy in copies[3:]:
                copy.wait()
        for s in range(sources_count):
            scatter(iteration, slot, s)
            exchange_b(s)
    for s in range(sources_count):
        out[0, s] = gather_field(s)
        sent_a(s)
        sent_b(s)

    def sent(k, carry):
        slab_copy(k).wait_send()
        return carry

    lax.fori_loop(1, group, sent, 0)


def born(depths, lats, incident, contrast, kernel):
    sources_count, part, length = incident.shape[1], incident.shape[3], incident.shape[4]
    period = 2 * length
    group = math.gcd(GROUP, depths)
    rows = period // (group * lats)
    half = rows // 2
    lanes = 4 * part
    block = jnp.bfloat16
    waves_y, forward_x, inverse_x = tables(length, lats)
    held = (incident, contrast, waves_y, forward_x, inverse_x)
    anywhere = pl.BlockSpec(memory_space=pl.ANY)
    return pl.pallas_call(
        functools.partial(born_kernel, depths, lats, group),
        out_shape=pltpu.VMEM(incident.shape, jnp.float32),
        in_specs=[anywhere] * 6,
        out_specs=pl.BlockSpec(memory_space=pltpu.VMEM),
        scratch_shapes=[pltpu.VMEM(a.shape, a.dtype) for a in held] + [
            pltpu.VMEM((group, depths, 2, rows, period), block),
            pltpu.VMEM((sources_count, group * lats, half, lanes), block),
            pltpu.VMEM((2, sources_count, depths, lats, half, lanes), block),
            pltpu.VMEM((sources_count, group, lats, half, lanes), block),
            pltpu.VMEM((sources_count, group * lats, half, lanes), block),
            pltpu.VMEM((depths, rows, 2 * period), jnp.float32),
            pltpu.VMEM((group, rows, 2 * period), jnp.float32),
            pltpu.SemaphoreType.DMA((len(held),)),
            pltpu.SemaphoreType.DMA((group,)),
            pltpu.SemaphoreType.DMA((group,)),
            pltpu.SemaphoreType.DMA((sources_count,)),
            pltpu.SemaphoreType.DMA((2, sources_count)),
            pltpu.SemaphoreType.DMA((sources_count,)),
            pltpu.SemaphoreType.DMA((sources_count,)),
        ],
        compiler_params=pltpu.CompilerParams(collective_id=0, has_side_effects=True),
        name="born",
    )(incident, contrast, kernel, waves_y, forward_x, inverse_x)


def solution(mesh):
    in_specs = (
        P("depth", None, None, "lat", None),
        P("depth", "lat", None),
        P("depth", None, None, "lat", None),
    )
    out_specs = P("depth", None, None, "lat", None)
    run = functools.partial(born, mesh.shape["depth"], mesh.shape["lat"])
    return jax.shard_map(run, mesh=mesh, in_specs=in_specs, out_specs=out_specs, check_vma=False)
```

```python
import functools
import math

import jax
import jax.numpy as jnp
import numpy as np
from jax import lax
from jax.experimental import pallas as pl
from jax.experimental.pallas import tpu as pltpu
from jax.sharding import PartitionSpec as P

ITERS = 3
GROUP = 4
MESH = pl.DeviceIdType.MESH


def dft(rows, columns, period):
    angles = (np.outer(np.arange(rows), np.arange(columns)) % period) * (2.0 * math.pi / period)
    return np.cos(angles), np.sin(angles)


def tables(length, lats):
    period = 2 * length
    part = length // lats
    cos_f, sin_f = dft(length, period, period)
    cos_i, sin_i = dft(period, length, period)
    waves_y = np.concatenate([cos_i, sin_i], axis=1)
    real_rows = np.concatenate([cos_f, -sin_f], axis=1).reshape(lats, part, 2 * period)
    imag_rows = np.concatenate([sin_f, cos_f], axis=1).reshape(lats, part, 2 * period)
    forward_x = np.stack([real_rows, imag_rows], axis=1).reshape(2 * length, 2 * period)
    to_real = np.concatenate([cos_i, -sin_i], axis=0).reshape(2 * period, lats, part)
    to_imag = np.concatenate([sin_i, cos_i], axis=0).reshape(2 * period, lats, part)
    inverse_x = np.stack([to_real, to_imag], axis=2).reshape(2 * period, 2 * length)
    return tuple(jnp.asarray(t, jnp.bfloat16) for t in (waves_y, forward_x, inverse_x))


def born_kernel(
    depths, lats, group,
    incident_hbm, contrast_hbm, green, waves_y_hbm, forward_x_hbm, inverse_x_hbm, out,
    incident, contrast, waves_y, forward_x, inverse_x,
    slabs, out_a, in_a, out_b, in_b, spectra, scattered,
    loads, slab_send, slab_recv, send_a, recv_a, send_b, recv_b,
):
    depth = lax.axis_index("depth")
    lat = lax.axis_index("lat")
    devices = depths * lats
    members = group * lats
    me = depth * lats + lat
    place = lax.rem(depth, group)
    first = depth - place
    half = out_a.shape[2]
    rows = 2 * half
    sources_count, _, part, length = incident.shape[1:]
    lanes = 2 * part
    period = 2 * length

    def peer(k):
        number = lax.rem(me + k, devices)
        return number // lats, lax.rem(number, lats)

    def member(k):
        number = lax.rem(place * lats + lat + k, members)
        return number // lats, lax.rem(number, lats)

    barrier = pltpu.get_barrier_semaphore()

    def greet(k, carry):
        pl.semaphore_signal(barrier, inc=1, device_id=peer(k), device_id_type=MESH)
        return carry

    lax.fori_loop(1, devices, greet, 0)

    pairs = (
        (contrast_hbm, contrast), (incident_hbm, incident), (waves_y_hbm, waves_y),
        (forward_x_hbm, forward_x), (inverse_x_hbm, inverse_x),
    )
    copies = [pltpu.make_async_copy(a, b, loads.at[n]) for n, (a, b) in enumerate(pairs)]
    own = pltpu.make_async_copy(
        green.at[0, :, :, pl.ds(pl.multiple_of(place * rows, rows), rows)],
        slabs.at[place],
        slab_recv.at[place],
    )
    for copy in copies:
        copy.start()
    own.start()

    def spread_along_y(s, field):
        driven = contrast[0][None] * field.reshape(2, part, length)
        turned = jnp.concatenate([driven[1:2], -driven[0:1]], axis=0)
        both = jnp.concatenate(
            [driven.reshape(lanes, length), turned.reshape(lanes, length)], axis=1
        ).astype(jnp.bfloat16)
        along_y = lax.dot_general(
            waves_y[...], both, (((1,), (1,)), ((), ())), preferred_element_type=jnp.float32
        ).reshape(members, 2, half, lanes)
        out_a[s] = jnp.concatenate([along_y[:, 0], along_y[:, 1]], axis=-1).astype(jnp.bfloat16)

    def exchange_a(slot, s):
        def start(d, l):
            pltpu.make_async_remote_copy(
                out_a.at[s, l * group + lax.rem(d, group)], in_a.at[slot, s, depth, lat],
                send_a.at[s], recv_a.at[slot, s],
                device_id=(d, l), device_id_type=MESH,
            ).start()

        def far(k, carry):
            d, l = member(lax.rem(k, members))
            start(lax.rem(first + (k // members + 1) * group, depths) + d, l)
            return carry

        def near(k, carry):
            d, l = member(k)
            start(first + d, l)
            return carry

        lax.fori_loop(0, devices - members, far, 0, unroll=members)
        lax.fori_loop(1, members, near, 0, unroll=True)
        pltpu.make_async_copy(
            out_a.at[s, lat * group + place], in_a.at[slot, s, depth, lat], recv_a.at[slot, s]
        ).start()

    def sent_a(s):
        block = in_a.at[0, s].reshape(devices, half, 2 * lanes).at[1:]
        pltpu.make_async_copy(block, block, send_a.at[s]).wait()

    def exchange_b(s):
        def send(k, carry):
            d, l = member(k)
            pltpu.make_async_remote_copy(
                out_b.at[s, d, l], in_b.at[s, lat * group + place], send_b.at[s], recv_b.at[s],
                device_id=(first + d, l), device_id_type=MESH,
            ).start()
            return carry

        lax.fori_loop(1, members, send, 0, unroll=True)
        pltpu.make_async_copy(
            out_b.at[s, place, lat], in_b.at[s, lat * group + place], recv_b.at[s]
        ).start()

    def sent_b(s):
        block = in_b.at[s, 1:]
        pltpu.make_async_copy(block, block, send_b.at[s]).wait()

    def slab_copy(k):
        d = lax.rem(place + k, group)
        return pltpu.make_async_remote_copy(
            green.at[0, :, :, pl.ds(pl.multiple_of(d * rows, rows), rows)],
            slabs.at[place], slab_send.at[d], slab_recv.at[place],
            device_id=(first + d, lat), device_id_type=MESH,
        )

    def couple(chains, wait_slabs):
        zero = jnp.zeros((rows, period), jnp.float32)

        def receive(k, carry):
            z = lax.rem(place + k, group)
            if wait_slabs:
                pltpu.make_async_copy(slabs.at[z], slabs.at[z], slab_recv.at[z]).wait()

            def add(s, w, sums):
                kern_real = slabs[z, w, 0].astype(jnp.float32)
                kern_imag = slabs[z, w, 1].astype(jnp.float32)
                spec_real = spectra[s, w, :, :period]
                spec_imag = spectra[s, w, :, period:]
                return (
                    sums[0] + (kern_real * spec_real - kern_imag * spec_imag),
                    sums[1] + (kern_real * spec_imag + kern_imag * spec_real),
                )

            for s in chains:
                real, imag = lax.fori_loop(0, depths, functools.partial(add, s), (zero, zero), unroll=8)
                scattered[s, z, :, :period] = real
                scattered[s, z, :, period:] = imag
            return carry

        lax.fori_loop(0, group, receive, 0)

    def spread_along_x(slot, s):
        pltpu.make_async_copy(in_a.at[slot, s], in_a.at[slot, s], recv_a.at[slot, s]).wait()
        blocks = [
            in_a[slot, s, :, l].astype(jnp.float32).reshape(depths * half, 2 * lanes)
            for l in range(lats)
        ]
        for h in range(2):
            along_y = jnp.concatenate(
                [b[:, h * lanes:(h + 1) * lanes] for b in blocks], axis=1
            ).astype(jnp.bfloat16)
            spectra[s, :, h * half:(h + 1) * half] = jnp.dot(
                along_y, forward_x[...], preferred_element_type=jnp.float32
            ).reshape(depths, half, 2 * period)

    def gather_along_x(iteration, s):
        along_x = jnp.dot(
            scattered[s].reshape(group * rows, 2 * period).astype(jnp.bfloat16),
            inverse_x[...],
            preferred_element_type=jnp.float32,
        )
        if iteration > 0:
            sent_b(s)
        for l in range(lats):
            mine = along_x[:, l * lanes:(l + 1) * lanes].reshape(group, 2, half, lanes)
            out_b[s, :, l] = jnp.concatenate([mine[:, 0], mine[:, 1]], axis=-1).astype(jnp.bfloat16)

    def gather_field(s):
        pltpu.make_async_copy(in_b.at[s], in_b.at[s], recv_b.at[s]).wait()
        blocks = in_b[s].astype(jnp.float32)
        along_x = jnp.stack(
            [blocks[:, :, :lanes], blocks[:, :, lanes:]], axis=1
        ).reshape(period, lanes).astype(jnp.bfloat16)
        turned = lax.dot_general(
            along_x, waves_y[...], (((0,), (0,)), ((), ())), preferred_element_type=jnp.float32
        )
        cosine = turned[:, :length].reshape(2, part, length)
        sine = turned[:, length:].reshape(2, part, length)
        sums = jnp.concatenate([cosine[0:1] - sine[1:2], cosine[1:2] + sine[0:1]], axis=0)
        return incident[0, s] + sums * (1.0 / float(period * period))

    for iteration in range(ITERS):
        slot = iteration % 2
        for s in range(sources_count):
            if iteration == 0:
                if s == 0:
                    for copy in copies[:3]:
                        copy.wait()
                field = incident[0, s]
            else:
                field = gather_field(s)
                sent_a(s)
            spread_along_y(s, field)
            if iteration > 0:
                exchange_a(slot, s)
        if iteration == 0:
            pl.semaphore_wait(barrier, devices - 1)
            def deal(k, carry):
                slab_copy(k).start()
                return carry

            for s in range(sources_count):
                exchange_a(slot, s)
                if s == 0:
                    lax.fori_loop(1, group, deal, 0)

            for copy in copies[3:]:
                copy.wait()
        if iteration == 0:
            for s in range(sources_count):
                spread_along_x(slot, s)
            couple(range(sources_count), True)
        for s in range(sources_count):
            if iteration > 0:
                spread_along_x(slot, s)
                couple((s,), False)
            gather_along_x(iteration, s)
            exchange_b(s)
    for s in range(sources_count):
        out[0, s] = gather_field(s)
        sent_a(s)
        sent_b(s)

    def sent(k, carry):
        slab_copy(k).wait_send()
        return carry

    lax.fori_loop(1, group, sent, 0)


def born(depths, lats, incident, contrast, kernel):
    sources_count, part, length = incident.shape[1], incident.shape[3], incident.shape[4]
    period = 2 * length
    group = math.gcd(GROUP, depths)
    rows = period // (group * lats)
    half = rows // 2
    lanes = 4 * part
    block = jnp.bfloat16
    waves_y, forward_x, inverse_x = tables(length, lats)
    held = (incident, contrast, waves_y, forward_x, inverse_x)
    anywhere = pl.BlockSpec(memory_space=pl.ANY)
    return pl.pallas_call(
        functools.partial(born_kernel, depths, lats, group),
        out_shape=pltpu.VMEM(incident.shape, jnp.float32),
        in_specs=[anywhere] * 6,
        out_specs=pl.BlockSpec(memory_space=pltpu.VMEM),
        scratch_shapes=[pltpu.VMEM(a.shape, a.dtype) for a in held] + [
            pltpu.VMEM((group, depths, 2, rows, period), block),
            pltpu.VMEM((sources_count, group * lats, half, lanes), block),
            pltpu.VMEM((2, sources_count, depths, lats, half, lanes), block),
            pltpu.VMEM((sources_count, group, lats, half, lanes), block),
            pltpu.VMEM((sources_count, group * lats, half, lanes), block),
            pltpu.VMEM((sources_count, depths, rows, 2 * period), jnp.float32),
            pltpu.VMEM((sources_count, group, rows, 2 * period), jnp.float32),
            pltpu.SemaphoreType.DMA((len(held),)),
            pltpu.SemaphoreType.DMA((group,)),
            pltpu.SemaphoreType.DMA((group,)),
            pltpu.SemaphoreType.DMA((sources_count,)),
            pltpu.SemaphoreType.DMA((2, sources_count)),
            pltpu.SemaphoreType.DMA((sources_count,)),
            pltpu.SemaphoreType.DMA((sources_count,)),
        ],
        compiler_params=pltpu.CompilerParams(collective_id=0, has_side_effects=True),
        name="born",
    )(incident, contrast, kernel, waves_y, forward_x, inverse_x)


def solution(mesh):
    in_specs = (
        P("depth", None, None, "lat", None),
        P("depth", "lat", None),
        P("depth", None, None, "lat", None),
    )
    out_specs = P("depth", None, None, "lat", None)
    run = functools.partial(born, mesh.shape["depth"], mesh.shape["lat"])
    return jax.shard_map(run, mesh=mesh, in_specs=in_specs, out_specs=out_specs, check_vma=False)
```
